32 devices in a mesh: row: 16 (over z, y, x), col: 2 (over core).
Axes of the slice: x: 2, y: 2, z: 4, core: 2. Of those that a mesh axis runs over, the one named last changes fastest.
Arguments:
- samples: bfloat16 [32768, 8192], P('row', 'col'), may hold values from -0.046875 to 0.046875
- targets: float32 [32768, 128], P('row'), may hold values from -6 to 6
- factor_inv: float32 [2, 4096, 4096], P('col', None, 'row'), may hold values from -1 to 1, as said below
Outputs:
- solution: float32 [8192, 128], P('col')
- residual: float32 [32768, 128], P('row')
The draws below stay inside these ranges and needn't reach their ends.
Inputs may be any that keep to these rules, and one draw needn't show every extreme that they name: Each factor_inv[j] is lower triangular with a positive diagonal.
All inputs are finite; a program needn't handle non-finite values.
Results may differ from the reference program's by a relative error of at most 0.0039.
Values sent between devices are 32-bit elements; how exact they have to be, the bound alone decides.
A program may use at most 128 MiB of HBM per device.

```python
import jax
import jax.numpy as jnp
from jax import lax

B = 4096
K = 128
ROUNDS = 3
NBLK = 2
FEAT = 8192
SAMPLES = 32768


def draw_factor_inv(key, part):
    key_low = jax.random.fold_in(key, 11)
    key_diag = jax.random.fold_in(key, 23)
    lower = jax.random.normal(key_low, (NBLK, B, B), jnp.float32) * (0.3 / jnp.sqrt(jnp.float32(B)))
    diag = jax.random.uniform(key_diag, (NBLK, B), jnp.float32, 0.5, 1.0)
    row_ids = lax.broadcasted_iota(jnp.int32, (B, B), 0)
    col_ids = lax.broadcasted_iota(jnp.int32, (B, B), 1)
    below = (row_ids > col_ids)[None, :, :]
    on_diag = (row_ids == col_ids)[None, :, :]
    return jnp.where(below, lower, 0.0) + jnp.where(on_diag, diag[:, :, None], 0.0)


def with_spikes(array, own_key, source, target, blocks, factor):
    def block_of(dim):
        return (jnp.arange(array.shape[dim]) // (array.shape[dim] // blocks)).reshape((-1,) + (1,) * (array.ndim - 1 - dim))

    one_side = jax.random.permutation(own_key, blocks)[block_of(target)]
    far = (block_of(target) + blocks // 2) % blocks
    return jnp.where((block_of(source) == one_side) | (block_of(source) == far), factor * array, array)


def block_levels(key, dims, split, smallest, top_value):
    gain = 1.0
    for position, blocks in split:
        draws = jax.random.uniform(jax.random.fold_in(jax.random.fold_in(key, 6), position), (blocks,), jnp.float32, smallest / len(split), top_value / len(split))
        gain = gain * jnp.repeat(jnp.exp(draws), dims[position] // blocks).reshape((-1,) + (1,) * (len(dims) - 1 - position))
    return gain


def centred(rng, extent, scale, reach, shards=(), dtype=jnp.bfloat16):
    values = jax.random.normal(rng, extent, jnp.float32) * scale
    if len(shards) > 0:
        values = block_levels(rng, extent, shards, -0.22, 0.18) * values
    return jnp.clip(values, min=-reach, max=reach).astype(dtype)


def heavy_noise(key, extent, spread, bound, cuts, heavy, held_as=jnp.bfloat16):
    array = spread * jax.random.normal(key, extent, jnp.float32)
    if cuts:
        array = array * block_levels(key, extent, cuts, -0.22, 0.18)
    return jnp.clip(with_spikes(array, jax.random.fold_in(key, 3), *heavy), -bound, bound).astype(held_as)


def setup_inputs(seed: int = 0) -> dict:
    arg_keys = jax.random.split(jax.random.key(seed), 4)
    samples = heavy_noise(arg_keys[0], (SAMPLES, FEAT), SAMPLES ** -0.5, 0.046875, ((0, 16), (1, 2)), (0, 1, 16, 2.0))
    targets = centred(arg_keys[1], (SAMPLES, K), 1.0, 6.0, ((0, 16),), jnp.float32)
    factor_inv = draw_factor_inv(jax.random.fold_in(arg_keys[3], 71), 0)
    return {"samples": samples, "targets": targets, "factor_inv": factor_inv}


ridge_weight = 0.5


def reference(samples, targets, factor_inv):
    residual = targets
    solution = [jnp.zeros((B, K), jnp.float32) for block in range(NBLK)]
    relaxation = 1.0 / NBLK
    for sweep in range(ROUNDS):
        res16 = residual.astype(jnp.bfloat16)
        total = jnp.zeros(residual.shape, jnp.float32)
        for block in range(NBLK):
            columns = samples[:, block * B:(block + 1) * B]
            grad = jnp.dot(columns.T, res16, preferred_element_type=jnp.float32) - ridge_weight * solution[block]
            image = jnp.dot(factor_inv[block], grad, precision=lax.Precision.HIGHEST)
            update = jnp.dot(factor_inv[block].T, image, precision=lax.Precision.HIGHEST)
            solution[block] = solution[block] + relaxation * update
            total = total + jnp.dot(columns, update.astype(jnp.bfloat16), preferred_element_type=jnp.float32)
        residual = residual - relaxation * total
    return jnp.concatenate(solution, axis=0), residual
```

```python
import functools

import jax
import jax.numpy as jnp
from jax import lax
from jax.experimental import pallas as pl
from jax.experimental.pallas import tpu as pltpu
from jax.sharding import PartitionSpec as P

ROUNDS = 3
PARTS = 4


ridge_weight = 0.5


def bit_orders(nbits):
    if nbits == 4:
        return [(3, 2, 1, 0), (2, 3, 0, 1), (1, 3, 2, 0), (0, 2, 3, 1)]
    return [tuple((nbits - 1 - p - t) % nbits for t in range(nbits)) for p in range(PARTS)]


def exchange_kernel(axis, nbits, reduce, gather, x_ref, out_ref, send_sem, recv_sem, *scratch):
    me = lax.axis_index(axis)
    bits = [lax.rem(lax.div(me, 2**b), 2) for b in range(nbits)]
    partner = [me + (1 - 2 * bits[b]) * 2**b for b in range(nbits)]
    orders = bit_orders(nbits)
    rows = (x_ref if not reduce else out_ref if not gather else x_ref).shape[-2] // PARTS
    span = [pl.ds(p * rows, rows) for p in range(PARTS)]

    def index(p, free, flip=None):
        lead = []
        for b in reversed(range(nbits)):
            if b in free:
                lead.append(slice(None))
            else:
                lead.append(1 - bits[b] if b == flip else bits[b])
        return tuple(lead) + (span[p], slice(None))

    def own(p):
        return index(p, ()) if gather else (span[p], slice(None))

    barrier = pltpu.get_barrier_semaphore()
    for b in range(nbits):
        pl.semaphore_signal(
            barrier, inc=1, device_id={axis: partner[b]}, device_id_type=pl.DeviceIdType.MESH
        )
    pl.semaphore_wait(barrier, nbits)

    def start(p, step, source, target, b):
        copy = pltpu.make_async_remote_copy(
            src_ref=source,
            dst_ref=target,
            send_sem=send_sem.at[p, step],
            recv_sem=recv_sem.at[p, step],
            device_id={axis: partner[b]},
            device_id_type=pl.DeviceIdType.MESH,
        )
        copy.start()
        return copy

    live = [None] * PARTS
    step = 0
    if reduce:
        acc, arrived = scratch[0], scratch[1:]

        def landing(p, t):
            return (slice(None),) * (nbits - 1 - t) + (span[p], slice(None))

        def add(p, t):
            live[p].wait()
            keep = index(p, orders[p][: nbits - 1 - t])
            source = x_ref if t == 0 else acc
            value = source[keep] + arrived[t][landing(p, t)]
            if t == nbits - 1:
                out_ref[own(p)] = value
            else:
                acc[keep] = value

        for t in range(nbits):
            for p in range(PARTS):
                if t > 0:
                    add(p, t - 1)
                b = orders[p][nbits - 1 - t]
                source = x_ref if t == 0 else acc
                live[p] = start(
                    p,
                    step,
                    source.at[index(p, orders[p][: nbits - 1 - t], b)],
                    arrived[t].at[landing(p, t)],
                    b,
                )
            step += 1
    for t in range(nbits if gather else 0):
        for p in range(PARTS):
            if t > 0:
                live[p].wait()
            elif reduce:
                add(p, nbits - 1)
            else:
                out_ref[own(p)] = x_ref[span[p], :]
            piece = out_ref.at[index(p, orders[p][:t])]
            live[p] = start(p, step, piece, piece, orders[p][t])
        step += 1
    for p in range(PARTS):
        if gather:
            live[p].wait()
        else:
            add(p, nbits - 1)


def exchange(x, axis, collective_id, reduce, gather):
    n = lax.axis_size(axis)
    nbits = n.bit_length() - 1
    width = x.shape[1]
    block = x.shape[0] // n if reduce else x.shape[0]
    whole = (2,) * nbits + (block, width)
    scratch = []
    if reduce:
        scratch.append(pltpu.VMEM(whole, jnp.float32))
        for t in range(nbits):
            scratch.append(pltpu.VMEM((2,) * (nbits - 1 - t) + (block, width), jnp.float32))
    steps = nbits * (int(reduce) + int(gather))
    out = pl.pallas_call(
        functools.partial(exchange_kernel, axis, nbits, reduce, gather),
        out_shape=jax.ShapeDtypeStruct(whole if gather else (block, width), jnp.float32),
        in_specs=[pl.BlockSpec(memory_space=pltpu.VMEM)],
        out_specs=pl.BlockSpec(memory_space=pltpu.VMEM),
        scratch_shapes=[
            pltpu.SemaphoreType.DMA((PARTS, steps)),
            pltpu.SemaphoreType.DMA((PARTS, steps)),
        ]
        + scratch,
        compiler_params=pltpu.CompilerParams(
            collective_id=collective_id, has_side_effects=True, vmem_limit_bytes=24 << 20
        ),
    )(x.reshape(whole) if reduce else x)
    return out.reshape(-1, width)


F32, BF16 = jnp.float32, jnp.bfloat16
MESH = pl.DeviceIdType.MESH
FEAT_TILE = 256
X_FIRST, Y_FIRST, X_THEN_Y, Y_THEN_X = (0, 2, 3, 1), (1, 2, 3, 0), (0, 1, 2, 3), (1, 0, 2, 3)
STREAMS = (
    ((X_FIRST, 0, 24), (Y_FIRST, 24, 24), (X_THEN_Y, 48, 8), (Y_THEN_X, 56, 8)),
    ((X_FIRST, 64, 24), (Y_FIRST, 88, 24), (X_THEN_Y, 112, 8), (Y_THEN_X, 120, 8)),
)
NBITS = 4
GROUPS = ((1, 1), (1, 0), (0, 1), (0, 0))


def dot(a, b, b_dim):
    return lax.dot_general(a, b, (((1,), (b_dim,)), ((), ())), preferred_element_type=F32)


def split(x):
    high = x.astype(BF16)
    return high, (x - high.astype(F32)).astype(BF16)


def fused_kernel(
    samples_hbm, factor_hbm, targets_ref, sol_ref, res_ref,
    rows_vmem, factor_f32, factor_hi, factor_lo, res16, grad, grad_in, term, term_in, image, update,
    change, change_in, load_sem, factor_sem, send_sem, recv_sem, core_send, core_recv,
):
    me = lax.axis_index("row")
    col = lax.axis_index("col")
    bits = [lax.rem(lax.div(me, 2**b), 2) for b in range(NBITS)]
    partner = [me + (1 - 2 * bits[b]) * 2**b for b in range(NBITS)]

    def block(z, dx, dy):
        lead = (z // 2, z % 2, 1 - bits[1] if dy else bits[1], 1 - bits[0] if dx else bits[0])
        return lead, ((lead[0] * 2 + lead[1]) * 2 + lead[2]) * 2 + lead[3]

    def load(flat):
        start = pl.multiple_of(flat * FEAT_TILE, FEAT_TILE)
        return pltpu.make_async_copy(
            samples_hbm.at[:, pl.ds(start, FEAT_TILE)], rows_vmem.at[flat], load_sem.at[flat]
        )

    order = [block(z, dx, dy) for dx, dy in GROUPS for z in range(4)]
    for _, flat in order:
        load(flat).start()
    factor_load = pltpu.make_async_copy(factor_hbm, factor_f32, factor_sem)
    factor_load.start()

    barrier = pltpu.get_barrier_semaphore()
    for b in range(NBITS):
        pl.semaphore_signal(barrier, inc=1, device_id={"row": partner[b]}, device_id_type=MESH)
    pl.semaphore_signal(barrier, inc=1, device_id={"col": 1 - col}, device_id_type=MESH)
    pl.semaphore_wait(barrier, NBITS + 1)

    res_ref[...] = targets_ref[...]
    res16[...] = targets_ref[...].astype(BF16)
    sol_ref[...] = jnp.zeros_like(sol_ref)

    def index(rows, free, flip=None):
        lead = []
        for b in reversed(range(NBITS)):
            if b in free:
                lead.append(slice(None))
            else:
                lead.append(1 - bits[b] if b == flip else bits[b])
        return tuple(lead) + (rows, slice(None))

    own = tuple(bits[b] for b in reversed(range(NBITS)))

    def remote(source, target, b, s, phase, p, t):
        copy = pltpu.make_async_remote_copy(
            src_ref=source, dst_ref=target,
            send_sem=send_sem.at[s, phase, p, t], recv_sem=recv_sem.at[s, phase, p, t],
            device_id={"row": partner[b]}, device_id_type=MESH,
        )
        copy.start()
        return copy

    def run_stream(s, rnd):
        parts = STREAMS[s]
        lo, hi = parts[0][1], parts[-1][1] + parts[-1][2]
        rows = slice(lo, hi)
        width = hi - lo
        live = [None] * len(parts)

        def scatter_start(p, buf, landing, phase, t):
            bit_order, off, size = parts[p]
            free = bit_order[t + 1 :]
            span = pl.ds(off, size)
            live[p] = remote(
                buf.at[index(span, free, bit_order[t])],
                landing[t].at[(slice(None),) * (NBITS - 1 - t) + (span, slice(None))],
                bit_order[t], s, phase, p, t,
            )

        def scatter_add(p, buf, landing, t):
            bit_order, off, size = parts[p]
            span = pl.ds(off, size)
            live[p].wait()
            keep = index(span, bit_order[t + 1 :])
            value = buf[keep] + landing[t][(slice(None),) * (NBITS - 1 - t) + (span, slice(None))]
            buf[keep] = value

        def scatter(produce, buf, landing, phase):
            for g, (dx, dy) in enumerate(GROUPS):
                produce(dx, dy)
                for p, (bit_order, _, _) in enumerate(parts):
                    if g == (1 if bit_order[0] == 0 else 2):
                        scatter_start(p, buf, landing, phase, 0)
                if g == 1:
                    yield
            for t in range(1, NBITS + 1):
                yield
                for p in range(len(parts)):
                    scatter_add(p, buf, landing, t - 1)
                    if t < NBITS:
                        scatter_start(p, buf, landing, phase, t)

        def gather(buf, phase, consume):
            for t in range(NBITS):
                if t > 0:
                    yield
                for p, (bit_order, off, size) in enumerate(parts):
                    if t > 0:
                        live[p].wait()
                    back = bit_order[::-1]
                    piece = buf.at[index(pl.ds(off, size), back[:t])]
                    live[p] = remote(piece, piece, back[t], s, phase, p, t)
            consume(0, 0)
            yield
            for p in range(len(parts)):
                live[p].wait()
            consume(1, 0)
            consume(0, 1)
            yield
            consume(1, 1)

        def make_grad(dx, dy):
            for z in range(4):
                lead, flat = block(z, dx, dy)
                if rnd == 0 and s == 0:
                    load(flat).wait()
                grad[lead + (rows, slice(None))] = dot(res16[rows, :], rows_vmem[flat], 0)

        yield from scatter(make_grad, grad, grad_in, 0)
        own_grad = grad[own + (rows, slice(None))]
        if rnd > 0:
            own_grad = own_grad - ridge_weight * sol_ref[own + (rows, slice(None))]
        g_hi, g_lo = split(own_grad)
        g_both = jnp.concatenate([g_hi, g_lo], axis=0)

        if rnd == 0 and s == 0:
            factor_load.wait()
            for i in range(16):
                span = slice(i * FEAT_TILE, (i + 1) * FEAT_TILE)
                f_hi, f_lo = split(factor_f32[span, :])
                factor_hi[i] = f_hi
                factor_lo[i] = f_lo

        def make_term(dx, dy):
            for z in range(4):
                lead, flat = block(z, dx, dy)
                both = dot(g_both, factor_hi[flat], 1)
                term[lead + (rows, slice(None))] = (
                    both[:width] + both[width:] + dot(g_hi, factor_lo[flat], 1)
                )

        yield from scatter(make_term, term, term_in, 1)
        image[own + (rows, slice(None))] = term[own + (rows, slice(None))]

        total = [jnp.zeros((width, FEAT_TILE), F32)]

        def use_image(dx, dy):
            for z in range(4):
                lead, flat = block(z, dx, dy)
                i_hi, i_lo = split(image[lead + (rows, slice(None))])
                both = dot(jnp.concatenate([i_hi, i_lo], axis=0), factor_hi[flat], 0)
                total[0] = total[0] + both[:width] + both[width:] + dot(i_hi, factor_lo[flat], 0)

        yield from gather(image, 2, use_image)
        update[own + (rows, slice(None))] = total[0]

        def use_update(dx, dy):
            acc = None if (dx, dy) == (0, 0) else change[rows, :]
            for z in range(4):
                lead, flat = block(z, dx, dy)
                value = update[lead + (rows, slice(None))]
                at = lead + (rows, slice(None))
                sol_ref[at] = sol_ref[at] + relaxation * value
                product = dot(value.astype(BF16), rows_vmem[flat], 1)
                acc = product if acc is None else acc + product
            change[rows, :] = acc

        yield from gather(update, 3, use_update)
        slot = rnd % 2
        copy = pltpu.make_async_remote_copy(
            src_ref=change.at[rows, :], dst_ref=change_in.at[slot, rows, :],
            send_sem=core_send.at[s, slot], recv_sem=core_recv.at[s, slot],
            device_id={"col": 1 - col}, device_id_type=MESH,
        )
        copy.start()
        yield
        copy.wait()
        residual = res_ref[rows, :] - relaxation * (change[rows, :] + change_in[slot, rows, :])
        res_ref[rows, :] = residual
        if rnd < ROUNDS - 1:
            res16[rows, :] = residual.astype(BF16)

    relaxation = 1.0 / lax.axis_size("col")

    def whole_stream(s):
        for rnd in range(ROUNDS):
            yield from run_stream(s, rnd)

    alive = [whole_stream(s) for s in range(len(STREAMS))]
    while alive:
        for g in list(alive):
            try:
                next(g)
            except StopIteration:
                alive.remove(g)


def fused(samples, targets, factor):
    count, width = samples.shape
    targets_t = targets.T
    lanes = targets_t.shape[0]
    blocks = (2,) * NBITS + (lanes, FEAT_TILE)
    n_blocks = width // FEAT_TILE
    landing = [pltpu.VMEM((2,) * (NBITS - 1 - t) + (lanes, FEAT_TILE), F32) for t in range(NBITS)]
    n_streams = len(STREAMS)
    n_parts = max(len(parts) for parts in STREAMS)
    vmem = pl.BlockSpec(memory_space=pltpu.VMEM)
    anywhere = pl.BlockSpec(memory_space=pl.ANY)
    copies = pltpu.SemaphoreType.DMA((n_streams, 4, n_parts, NBITS))
    sol, res = pl.pallas_call(
        fused_kernel,
        out_shape=(
            jax.ShapeDtypeStruct(blocks, F32),
            jax.ShapeDtypeStruct(targets_t.shape, F32),
        ),
        in_specs=[anywhere, anywhere, vmem],
        out_specs=(vmem, vmem),
        scratch_shapes=[
            pltpu.VMEM((n_blocks, count, FEAT_TILE), BF16),
            pltpu.VMEM(factor.shape, F32),
            pltpu.VMEM((n_blocks, FEAT_TILE, FEAT_TILE), BF16),
            pltpu.VMEM((n_blocks, FEAT_TILE, FEAT_TILE), BF16),
            pltpu.VMEM((lanes, count), BF16),
            pltpu.VMEM(blocks, F32),
            landing,
            pltpu.VMEM(blocks, F32),
            landing,
            pltpu.VMEM(blocks, F32),
            pltpu.VMEM(blocks, F32),
            pltpu.VMEM((lanes, count), F32),
            pltpu.VMEM((2, lanes, count), F32),
            pltpu.SemaphoreType.DMA((n_blocks,)),
            pltpu.SemaphoreType.DMA(()),
            copies,
            copies,
            pltpu.SemaphoreType.DMA((n_streams, 2)),
            pltpu.SemaphoreType.DMA((n_streams, 2)),
        ],
        compiler_params=pltpu.CompilerParams(
            collective_id=0, has_side_effects=True, vmem_limit_bytes=58 << 20
        ),
    )(samples, factor, targets_t)
    solution = jnp.swapaxes(sol.reshape(n_blocks, lanes, FEAT_TILE), 1, 2).reshape(width, lanes)
    return solution, res.T


def run_group(samples, residual, inverse, own_rows, offset, relaxation):
    solution = jnp.zeros((samples.shape[1], residual.shape[1]), jnp.float32)
    for sweep in range(ROUNDS):
        res16 = residual.astype(jnp.bfloat16)
        part_grad = jnp.einsum("rb,rk->bk", samples, res16, preferred_element_type=jnp.float32)
        own_solution = lax.dynamic_slice_in_dim(solution, offset, own_rows, 0)
        grad_own = exchange(part_grad, "row", 0, True, False) - ridge_weight * own_solution
        term = jnp.dot(inverse, grad_own, precision=lax.Precision.HIGH)
        image = exchange(term, "row", 1, True, True)
        update_own = jnp.einsum("bc,bk->ck", inverse, image, precision=lax.Precision.HIGH)
        update = exchange(update_own, "row", 2, False, True)
        solution = solution + relaxation * update
        change = jnp.dot(samples, update.astype(jnp.bfloat16), preferred_element_type=jnp.float32)
        residual = residual - relaxation * exchange(change, "col", 3, True, True)
    return (solution, residual)


def per_device(samples, targets, factor_inv):
    inverse = factor_inv[0]
    if lax.axis_size("row") == 2**NBITS and inverse.shape[1] == FEAT_TILE and lax.axis_size("col") == 2:
        return fused(samples, targets, inverse)
    own_rows = inverse.shape[1]
    offset = lax.axis_index("row") * own_rows
    relaxation = 1.0 / lax.axis_size("col")
    solution, residual = run_group(samples, targets, inverse, own_rows, offset, relaxation)
    return (solution, residual)


def solution(mesh):
    in_specs = (P("row", "col"), P("row", None), P("col", None, "row"))
    out_specs = (P("col", None), P("row", None))
    return jax.shard_map(
        per_device, mesh=mesh, in_specs=in_specs, out_specs=out_specs, check_vma=False
    )
```

```python
import functools

import jax
import jax.numpy as jnp
from jax import lax
from jax.experimental import pallas as pl
from jax.experimental.pallas import tpu as pltpu
from jax.sharding import PartitionSpec as P

ROUNDS = 3
PARTS = 4


ridge_weight = 0.5


def bit_orders(nbits):
    if nbits == 4:
        return [(3, 2, 1, 0), (2, 3, 0, 1), (1, 3, 2, 0), (0, 2, 3, 1)]
    return [tuple((nbits - 1 - p - t) % nbits for t in range(nbits)) for p in range(PARTS)]


def exchange_kernel(axis, nbits, reduce, gather, x_ref, out_ref, send_sem, recv_sem, *scratch):
    me = lax.axis_index(axis)
    bits = [lax.rem(lax.div(me, 2**b), 2) for b in range(nbits)]
    partner = [me + (1 - 2 * bits[b]) * 2**b for b in range(nbits)]
    orders = bit_orders(nbits)
    rows = (x_ref if not reduce else out_ref if not gather else x_ref).shape[-2] // PARTS
    span = [pl.ds(p * rows, rows) for p in range(PARTS)]

    def index(p, free, flip=None):
        lead = []
        for b in reversed(range(nbits)):
            if b in free:
                lead.append(slice(None))
            else:
                lead.append(1 - bits[b] if b == flip else bits[b])
        return tuple(lead) + (span[p], slice(None))

    def own(p):
        return index(p, ()) if gather else (span[p], slice(None))

    barrier = pltpu.get_barrier_semaphore()
    for b in range(nbits):
        pl.semaphore_signal(
            barrier, inc=1, device_id={axis: partner[b]}, device_id_type=pl.DeviceIdType.MESH
        )
    pl.semaphore_wait(barrier, nbits)

    def start(p, step, source, target, b):
        copy = pltpu.make_async_remote_copy(
            src_ref=source,
            dst_ref=target,
            send_sem=send_sem.at[p, step],
            recv_sem=recv_sem.at[p, step],
            device_id={axis: partner[b]},
            device_id_type=pl.DeviceIdType.MESH,
        )
        copy.start()
        return copy

    live = [None] * PARTS
    step = 0
    if reduce:
        acc, arrived = scratch[0], scratch[1:]

        def landing(p, t):
            return (slice(None),) * (nbits - 1 - t) + (span[p], slice(None))

        def add(p, t):
            live[p].wait()
            keep = index(p, orders[p][: nbits - 1 - t])
            source = x_ref if t == 0 else acc
            value = source[keep] + arrived[t][landing(p, t)]
            if t == nbits - 1:
                out_ref[own(p)] = value
            else:
                acc[keep] = value

        for t in range(nbits):
            for p in range(PARTS):
                if t > 0:
                    add(p, t - 1)
                b = orders[p][nbits - 1 - t]
                source = x_ref if t == 0 else acc
                live[p] = start(
                    p,
                    step,
                    source.at[index(p, orders[p][: nbits - 1 - t], b)],
                    arrived[t].at[landing(p, t)],
                    b,
                )
            step += 1
    for t in range(nbits if gather else 0):
        for p in range(PARTS):
            if t > 0:
                live[p].wait()
            elif reduce:
                add(p, nbits - 1)
            else:
                out_ref[own(p)] = x_ref[span[p], :]
            piece = out_ref.at[index(p, orders[p][:t])]
            live[p] = start(p, step, piece, piece, orders[p][t])
        step += 1
    for p in range(PARTS):
        if gather:
            live[p].wait()
        else:
            add(p, nbits - 1)


def exchange(x, axis, collective_id, reduce, gather):
    n = lax.axis_size(axis)
    nbits = n.bit_length() - 1
    width = x.shape[1]
    block = x.shape[0] // n if reduce else x.shape[0]
    whole = (2,) * nbits + (block, width)
    scratch = []
    if reduce:
        scratch.append(pltpu.VMEM(whole, jnp.float32))
        for t in range(nbits):
            scratch.append(pltpu.VMEM((2,) * (nbits - 1 - t) + (block, width), jnp.float32))
    steps = nbits * (int(reduce) + int(gather))
    out = pl.pallas_call(
        functools.partial(exchange_kernel, axis, nbits, reduce, gather),
        out_shape=jax.ShapeDtypeStruct(whole if gather else (block, width), jnp.float32),
        in_specs=[pl.BlockSpec(memory_space=pltpu.VMEM)],
        out_specs=pl.BlockSpec(memory_space=pltpu.VMEM),
        scratch_shapes=[
            pltpu.SemaphoreType.DMA((PARTS, steps)),
            pltpu.SemaphoreType.DMA((PARTS, steps)),
        ]
        + scratch,
        compiler_params=pltpu.CompilerParams(
            collective_id=collective_id, has_side_effects=True, vmem_limit_bytes=24 << 20
        ),
    )(x.reshape(whole) if reduce else x)
    return out.reshape(-1, width)


F32, BF16 = jnp.float32, jnp.bfloat16
MESH = pl.DeviceIdType.MESH
FEAT_TILE = 256
NBITS = 4
STREAMS = ((0, 64), (64, 64))
SCATTER = (((0, 1, 2, 3), 16), ((1, 0, 2, 3), 16), ((0, 2, 3, 1), 8), ((1, 2, 3, 0), 8), ((2, 0, 1, 3), 8), ((2, 1, 0, 3), 8))
REDUCE = (((0, 1, 2, 3), (2, 1, 0), 16), ((1, 0, 2, 3), (2, 0, 1), 16), ((0, 2, 3, 1), (3, 2, 0), 8), ((1, 2, 3, 0), (3, 2, 1), 8), ((2, 0, 1, 3), (1, 0, 2), 8), ((2, 1, 0, 3), (0, 1, 2), 8))
GATHER = (((3, 2, 1, 0), 16), ((3, 2, 0, 1), 16), ((1, 3, 2, 0), 8), ((0, 3, 2, 1), 8), ((3, 1, 0, 2), 8), ((3, 0, 1, 2), 8))
SCHEDULE = (
    0, 0, 0, 0, 10, 10, 10, 1, 10, 5, 2, 3, 6, 4, 11, 12, 15, 13, 5, 14, 16, 3, 2, 1, 4, 6, 13, 12,
    14, 11, 15, 5, 3, 16, 2, 6, 4, 1, 13, 15, 14, 3, 12, 5, 16, 4, 11, 2, 6, 13, 1, 0, 0, 0, 0, 14,
    0, 0, 15, 12, 16, 11, 0, 0, 0, 0, 10, 10, 10, 10, 10, 10, 10, 10, 10, 10, 5, 1, 2, 6, 3, 4, 15,
    16, 11, 12, 3, 4, 13, 14, 5, 1, 2, 6, 15, 3, 16, 4, 13, 12, 11, 14, 5, 1, 6, 15, 2, 3, 16, 4,
    13, 12, 14, 5, 11, 13, 1, 6, 14, 15, 5, 2, 3, 6, 1, 16, 15, 5, 4, 12, 2, 6, 16, 11, 15, 3, 1,
    13, 0, 14, 5, 16, 4, 2, 0, 0, 0, 0, 12, 3, 6, 0, 0, 11, 4, 15, 1, 13, 14, 12, 2, 0, 0, 16, 0,
    0, 0, 0, 11, 0, 10, 10, 10, 10, 10, 10, 13, 10, 14, 4, 1, 2, 12, 10, 5, 3, 10, 6, 10, 11, 10,
    10, 10, 4, 1, 10, 5, 2, 6, 3, 13, 14, 11, 12, 5, 4, 1, 15, 16, 0, 6, 3, 2, 0, 0, 0, 13, 14, 11,
    4, 12, 4, 5, 0, 1, 15, 5, 6, 0, 1, 2, 16, 6, 3, 13, 2, 3, 0, 0, 0, 14, 11, 12, 0, 0, 0, 0, 15,
    0, 16, 13, 13, 0, 0, 0, 0, 0, 14, 15, 14, 10, 10, 10, 11, 10, 10, 15, 12, 16, 10, 11, 16, 12,
    10, 10, 10, 10, 10, 10, 10, 10, 10, 10, 10, 10, 10, 0, 0, 0, 0, 10, 10, 10, 1, 5, 2, 3, 6, 4,
    10, 11, 3, 12, 4, 13, 5, 14, 15, 2, 1, 3, 6, 16, 4, 12, 13, 11, 15, 14, 5, 2, 3, 6, 1, 4, 16,
    12, 13, 15, 14, 5, 11, 2, 16, 6, 1, 13, 0, 0, 0, 0, 0, 0, 12, 14, 0, 15, 0, 0, 11, 16, 0, 10,
    10, 10, 10, 10, 10, 10, 10, 10, 10, 5, 1, 2, 6, 3, 4, 15, 16, 11, 12, 3, 4, 13, 14, 5, 1, 2,
    6, 15, 3, 16, 4, 13, 12, 14, 11, 5, 1, 6, 15, 2, 3, 16, 4, 13, 14, 12, 5, 11, 1, 13, 6, 14, 15,
    5, 2, 3, 6, 1, 16, 15, 5, 4, 12, 2, 6, 16, 11, 15, 3, 1, 13, 0, 14, 5, 16, 4, 2, 0, 0, 0, 0,
    12, 3, 6, 0, 0, 11, 4, 15, 1, 13, 14, 12, 2, 0, 0, 16, 0, 0, 0, 0, 11, 0, 10, 10, 10, 10, 10,
    10, 13, 10, 14, 4, 1, 2, 12, 10, 5, 3, 10, 6, 10, 11, 10, 10, 10, 4, 1, 10, 5, 2, 6, 3, 13, 14,
    11, 12, 5, 4, 1, 15, 16, 0, 6, 3, 2, 0, 0, 0, 13, 14, 11, 4, 12, 4, 5, 0, 1, 15, 5, 6, 0, 1,
    2, 16, 6, 3, 13, 2, 3, 0, 0, 0, 14, 11, 12, 0, 0, 0, 0, 15, 0, 16, 13, 13, 0, 0, 0, 0, 0, 14,
    15, 14, 10, 10, 10, 11, 10, 10, 15, 12, 16, 10, 11, 16, 12, 10, 10, 10, 10, 10, 10, 10, 10, 10,
    10, 10, 10, 10, 0, 0, 0, 0, 10, 10, 10, 1, 5, 2, 3, 6, 4, 10, 11, 3, 12, 4, 13, 5, 14, 15, 2,
    1, 3, 6, 16, 4, 12, 13, 11, 15, 14, 5, 2, 3, 6, 1, 4, 16, 12, 13, 15, 14, 5, 11, 2, 16, 6, 1,
    13, 0, 0, 0, 0, 0, 0, 12, 14, 0, 15, 0, 0, 11, 16, 0, 10, 10, 10, 10, 10, 10, 10, 10, 10, 10,
    5, 1, 2, 6, 3, 4, 15, 16, 11, 12, 3, 4, 13, 14, 5, 1, 2, 6, 15, 3, 16, 4, 13, 12, 14, 11, 5,
    1, 6, 15, 2, 3, 16, 4, 13, 14, 12, 5, 11, 1, 13, 6, 14, 15, 5, 2, 3, 6, 1, 16, 15, 5, 4, 12,
    2, 6, 16, 11, 15, 3, 1, 13, 0, 14, 5, 16, 4, 2, 0, 0, 0, 0, 12, 3, 6, 0, 0, 11, 4, 15, 1, 13,
    14, 12, 2, 0, 0, 16, 0, 0, 0, 0, 11, 0, 10, 10, 10, 10, 10, 10, 13, 10, 14, 4, 1, 2, 12, 10,
    5, 3, 10, 6, 10, 11, 10, 10, 10, 4, 1, 10, 5, 2, 6, 3, 13, 14, 11, 12, 5, 4, 1, 15, 16, 0, 6,
    3, 2, 0, 0, 0, 13, 14, 11, 4, 12, 4, 5, 0, 1, 15, 5, 6, 0, 1, 2, 16, 6, 3, 13, 2, 3, 0, 0, 0,
    14, 11, 12, 0, 0, 0, 0, 15, 0, 16, 13, 13, 0, 0, 0, 0, 0, 14, 15, 14, 10, 10, 10, 11, 10, 10,
    15, 12, 16, 10, 11, 16, 12, 10, 10, 10, 10, 10, 10, 10, 10, 10, 10, 10, 10, 10, 0, 10,
)
MADE = ((1, 1), (1, 0), (0, 1), (0, 0))
READY = (1, 2, 3, 3)
USED = ((0, 0), (0, 1), (1, 0), (1, 1))


def dot(a, b, b_dim):
    return lax.dot_general(a, b, (((1,), (b_dim,)), ((), ())), preferred_element_type=F32)


def split(x):
    high = x.astype(BF16)
    return high, (x - high.astype(F32)).astype(BF16)


def needed(last_bit, dx, dy, halves):
    if last_bit == 0:
        return 1 if not dx else 2 if halves and not dy else 3
    if last_bit == 1:
        return 1 if not dy else 2 if halves and not dx else 3
    return 2 if halves and not dx else 3


def fused_kernel(
    samples_hbm, factor_hbm, targets_ref, sol_ref, res_ref,
    rows_vmem, factor_f32, factor_hi, factor_lo, res16, grad, grad_in, term, term_in, image, update,
    change, change_in, load_sem, factor_sem, send_sem, recv_sem, core_send, core_recv,
):
    me = lax.axis_index("row")
    col = lax.axis_index("col")
    bits = [lax.rem(lax.div(me, 2**b), 2) for b in range(NBITS)]
    partner = [me + (1 - 2 * bits[b]) * 2**b for b in range(NBITS)]
    relaxation = 1.0 / lax.axis_size("col")

    def block(z, dx, dy):
        lead = (z // 2, z % 2, 1 - bits[1] if dy else bits[1], 1 - bits[0] if dx else bits[0])
        return lead, ((lead[0] * 2 + lead[1]) * 2 + lead[2]) * 2 + lead[3]

    def load(flat):
        start = pl.multiple_of(flat * FEAT_TILE, FEAT_TILE)
        return pltpu.make_async_copy(
            samples_hbm.at[:, pl.ds(start, FEAT_TILE)], rows_vmem.at[flat], load_sem.at[flat]
        )

    for dx, dy in MADE:
        for z in range(4):
            load(block(z, dx, dy)[1]).start()
    factor_load = pltpu.make_async_copy(factor_hbm, factor_f32, factor_sem)
    factor_load.start()

    barrier = pltpu.get_barrier_semaphore()
    for b in range(NBITS):
        pl.semaphore_signal(barrier, inc=1, device_id={"row": partner[b]}, device_id_type=MESH)
    pl.semaphore_signal(barrier, inc=1, device_id={"col": 1 - col}, device_id_type=MESH)

    for i in range(0, targets_ref.shape[0], FEAT_TILE):
        tile = targets_ref[i : i + FEAT_TILE, :].T
        res_ref[:, i : i + FEAT_TILE] = tile
        res16[:, i : i + FEAT_TILE] = tile.astype(BF16)
    sol_ref[...] = jnp.zeros_like(sol_ref)
    pl.semaphore_wait(barrier, NBITS + 1)

    def index(rows, free, flip=None, halves=None):
        lead = []
        for b in reversed(range(NBITS)):
            if halves is not None and b == halves[0]:
                lead.append(1 - bits[b] if halves[1] else bits[b])
            elif b in free:
                lead.append(slice(None))
            else:
                lead.append(1 - bits[b] if b == flip else bits[b])
        return tuple(lead) + (rows, slice(None))

    own = tuple(bits[b] for b in reversed(range(NBITS)))

    def remote(source, target, b, s, phase, p, t):
        copy = pltpu.make_async_remote_copy(
            src_ref=source, dst_ref=target,
            send_sem=send_sem.at[s, phase, p, t], recv_sem=recv_sem.at[s, phase, p, t],
            device_id={"row": partner[b]}, device_id_type=MESH,
        )
        copy.start()
        return copy

    def landed(free, span):
        return (slice(None),) * len(free) + (span, slice(None))

    threads = {}
    done = set()

    def spawn(name, thread):
        threads[name] = thread
        resume(name)

    def resume(name):
        try:
            next(threads[name])
        except StopIteration:
            del threads[name]

    def halve(buf, landing, order, span, s, phase, p, t):
        free = order[t + 1 :]
        return remote(
            buf.at[index(span, free, order[t])], landing[t].at[landed(free, span)], order[t], s, phase, p, t
        )

    def add(buf, landing, order, span, t):
        free = order[t + 1 :]
        keep = index(span, free)
        buf[keep] = buf[keep] + landing[t][landed(free, span)]

    def scatter_part(s, rnd, p, order, span, copy):
        for t in range(NBITS):
            yield
            copy.wait()
            add(grad, grad_in, order, span, t)
            if t < NBITS - 1:
                copy = halve(grad, grad_in, order, span, s, 0, p, t + 1)
        done.add((s, rnd, 0, p))

    def reduce_part(s, rnd, p, order, rest, span, copy):
        last = order[NBITS - 1 :]
        for t in range(NBITS - 1):
            yield
            copy.wait()
            add(term, term_in, order, span, t)
            if t < NBITS - 2:
                copy = halve(term, term_in, order, span, s, 1, p, t + 1)
        pair = index(span, last)
        copy = remote(term.at[pair], term_in[NBITS - 1].at[landed(last, span)], last[0], s, 1, p, NBITS - 1)
        yield
        copy.wait()
        image[pair] = term[pair] + term_in[NBITS - 1][landed(last, span)]
        for u, b in enumerate(rest):
            piece = image.at[index(span, last + rest[:u])]
            copy = remote(piece, piece, b, s, 2, p, u)
            if u == len(rest) - 1:
                done.add((s, rnd, 2, p, 1))
            yield
            copy.wait()
        done.add((s, rnd, 2, p, 3))

    def gather_part(s, rnd, p, order, span):
        for t in range(NBITS - 1):
            piece = update.at[index(span, order[:t])]
            copy = remote(piece, piece, order[t], s, 3, p, t)
            yield
            copy.wait()
        last = order[NBITS - 1]
        across = 1 if last == 0 else 0
        copies = []
        for h in range(2):
            piece = update.at[index(span, order[: NBITS - 1], None, (across, h))]
            copies.append(remote(piece, piece, last, s, 3, p, NBITS - 1 + h))
        done.add((s, rnd, 3, p, 1))
        for h in range(2):
            yield
            copies[h].wait()
            done.add((s, rnd, 3, p, 2 + h))

    def need(flag):
        assert flag in done

    def stream(s, rnd):
        lo, width = STREAMS[s]
        rows = slice(lo, lo + width)

        def placed(parts):
            out, at = [], lo
            for part in parts:
                out.append(part[:-1] + (pl.ds(at, part[-1]),))
                at += part[-1]
            return out

        def await_group(parts, phase, seen, dx, dy, halves):
            for p, part in enumerate(parts):
                event = needed(part[-2][-1], dx, dy, halves)
                if (p, event) not in seen:
                    seen.add((p, event))
                    yield
                    need((s, rnd, phase, p, event))

        for g, (dx, dy) in enumerate(MADE):
            for z in range(4):
                lead, flat = block(z, dx, dy)
                if rnd == 0 and s == 0:
                    load(flat).wait()
                grad[lead + (rows, slice(None))] = dot(res16[rows, :], rows_vmem[flat], 0)
            for p, (order, span) in enumerate(placed(SCATTER)):
                if READY[order[0]] == g:
                    copy = halve(grad, grad_in, order, span, s, 0, p, 0)
                    spawn((s, p), scatter_part(s, rnd, p, order, span, copy))
            if g < 3:
                yield
        for p in range(len(SCATTER)):
            yield
            need((s, rnd, 0, p))
        own_grad = grad[own + (rows, slice(None))]
        if rnd > 0:
            own_grad = own_grad - ridge_weight * sol_ref[own + (rows, slice(None))]
        g_hi, g_lo = split(own_grad)
        g_both = jnp.concatenate([g_hi, g_lo], axis=0)
        if rnd == 0 and s == 0:
            factor_load.wait()
            for i in range(16):
                f_hi, f_lo = split(factor_f32[i * FEAT_TILE : (i + 1) * FEAT_TILE, :])
                factor_hi[i] = f_hi
                factor_lo[i] = f_lo

        for g, (dx, dy) in enumerate(MADE):
            for z in range(4):
                lead, flat = block(z, dx, dy)
                both = dot(g_both, factor_hi[flat], 1)
                term[lead + (rows, slice(None))] = (
                    both[:width] + both[width:] + dot(g_hi, factor_lo[flat], 1)
                )
            for p, (order, rest, span) in enumerate(placed(REDUCE)):
                if READY[order[0]] == g:
                    copy = halve(term, term_in, order, span, s, 1, p, 0)
                    spawn((s, p), reduce_part(s, rnd, p, order, rest, span, copy))
            if g < 3:
                yield

        seen = set()
        total = jnp.zeros((width, FEAT_TILE), F32)
        for dx, dy in USED:
            yield
            yield from await_group(placed(REDUCE), 2, seen, dx, dy, False)
            for z in range(4):
                lead, flat = block(z, dx, dy)
                i_hi, i_lo = split(image[lead + (rows, slice(None))])
                both = dot(jnp.concatenate([i_hi, i_lo], axis=0), factor_hi[flat], 0)
                total = total + both[:width] + both[width:] + dot(i_hi, factor_lo[flat], 0)
        update[own + (rows, slice(None))] = total

        for p, (order, span) in enumerate(placed(GATHER)):
            spawn((s, p), gather_part(s, rnd, p, order, span))
        seen = set()
        for dx, dy in USED:
            yield
            yield from await_group(placed(GATHER), 3, seen, dx, dy, True)
            acc = None if (dx, dy) == USED[0] else change[rows, :]
            for z in range(4):
                lead, flat = block(z, dx, dy)
                at = lead + (rows, slice(None))
                value = update[at]
                sol_ref[at] = sol_ref[at] + relaxation * value
                product = dot(value.astype(BF16), rows_vmem[flat], 1)
                acc = product if acc is None else acc + product
            change[rows, :] = acc

        slot = rnd % 2
        copy = pltpu.make_async_remote_copy(
            src_ref=change.at[rows, :], dst_ref=change_in.at[slot, rows, :],
            send_sem=core_send.at[s, slot], recv_sem=core_recv.at[s, slot],
            device_id={"col": 1 - col}, device_id_type=MESH,
        )
        copy.start()
        yield
        copy.wait()
        residual = res_ref[rows, :] - relaxation * (change[rows, :] + change_in[slot, rows, :])
        res_ref[rows, :] = residual
        if rnd < ROUNDS - 1:
            res16[rows, :] = residual.astype(BF16)

    def whole(s):
        for rnd in range(ROUNDS):
            yield from stream(s, rnd)

    for s in range(len(STREAMS)):
        threads[(s,)] = whole(s)
    for number in SCHEDULE:
        s, p = divmod(number, 10)
        resume((s, p - 1) if p else (s,))
    assert not threads


def fused(samples, targets, factor):
    count, width = samples.shape
    lanes = targets.shape[1]
    blocks = (2,) * NBITS + (lanes, FEAT_TILE)
    n_blocks = width // FEAT_TILE

    def landing(sizes):
        return [pltpu.VMEM((2,) * free + (lanes, FEAT_TILE), F32) for free in sizes]

    n_streams = len(STREAMS)
    n_parts = max(len(SCATTER), len(REDUCE), len(GATHER))
    vmem = pl.BlockSpec(memory_space=pltpu.VMEM)
    anywhere = pl.BlockSpec(memory_space=pl.ANY)
    copies = pltpu.SemaphoreType.DMA((n_streams, 4, n_parts, NBITS + 1))
    sol, res = pl.pallas_call(
        fused_kernel,
        out_shape=(
            jax.ShapeDtypeStruct(blocks, F32),
            jax.ShapeDtypeStruct((lanes, count), F32),
        ),
        in_specs=[anywhere, anywhere, vmem],
        out_specs=(vmem, vmem),
        scratch_shapes=[
            pltpu.VMEM((n_blocks, count, FEAT_TILE), BF16),
            pltpu.VMEM(factor.shape, F32),
            pltpu.VMEM((n_blocks, FEAT_TILE, FEAT_TILE), BF16),
            pltpu.VMEM((n_blocks, FEAT_TILE, FEAT_TILE), BF16),
            pltpu.VMEM((lanes, count), BF16),
            pltpu.VMEM(blocks, F32),
            landing((3, 2, 1, 0)),
            pltpu.VMEM(blocks, F32),
            landing((3, 2, 1, 1)),
            pltpu.VMEM(blocks, F32),
            pltpu.VMEM(blocks, F32),
            pltpu.VMEM((lanes, count), F32),
            pltpu.VMEM((2, lanes, count), F32),
            pltpu.SemaphoreType.DMA((n_blocks,)),
            pltpu.SemaphoreType.DMA(()),
            copies,
            copies,
            pltpu.SemaphoreType.DMA((n_streams, 2)),
            pltpu.SemaphoreType.DMA((n_streams, 2)),
        ],
        compiler_params=pltpu.CompilerParams(
            collective_id=0, has_side_effects=True, vmem_limit_bytes=58 << 20
        ),
    )(samples, factor, targets)
    solution = jnp.swapaxes(sol.reshape(n_blocks, lanes, FEAT_TILE), 1, 2).reshape(width, lanes)
    return solution, res.T


def run_group(samples, residual, inverse, own_rows, offset, relaxation):
    solution = jnp.zeros((samples.shape[1], residual.shape[1]), jnp.float32)
    for sweep in range(ROUNDS):
        res16 = residual.astype(jnp.bfloat16)
        part_grad = jnp.einsum("rb,rk->bk", samples, res16, preferred_element_type=jnp.float32)
        own_solution = lax.dynamic_slice_in_dim(solution, offset, own_rows, 0)
        grad_own = exchange(part_grad, "row", 0, True, False) - ridge_weight * own_solution
        term = jnp.dot(inverse, grad_own, precision=lax.Precision.HIGH)
        image = exchange(term, "row", 1, True, True)
        update_own = jnp.einsum("bc,bk->ck", inverse, image, precision=lax.Precision.HIGH)
        update = exchange(update_own, "row", 2, False, True)
        solution = solution + relaxation * update
        change = jnp.dot(samples, update.astype(jnp.bfloat16), preferred_element_type=jnp.float32)
        residual = residual - relaxation * exchange(change, "col", 3, True, True)
    return (solution, residual)


def per_device(samples, targets, factor_inv):
    inverse = factor_inv[0]
    if lax.axis_size("row") == 2**NBITS and inverse.shape[1] == FEAT_TILE and lax.axis_size("col") == 2:
        return fused(samples, targets, inverse)
    own_rows = inverse.shape[1]
    offset = lax.axis_index("row") * own_rows
    relaxation = 1.0 / lax.axis_size("col")
    solution, residual = run_group(samples, targets, inverse, own_rows, offset, relaxation)
    return (solution, residual)


def solution(mesh):
    in_specs = (P("row", "col"), P("row", None), P("col", None, "row"))
    out_specs = (P("col", None), P("row", None))
    return jax.shard_map(
        per_device, mesh=mesh, in_specs=in_specs, out_specs=out_specs, check_vma=False
    )
```

```python
import functools

import jax
import jax.numpy as jnp
from jax import lax
from jax.experimental import pallas as pl
from jax.experimental.pallas import tpu as pltpu
from jax.sharding import PartitionSpec as P

ROUNDS = 3
PARTS = 4


ridge_weight = 0.5


def bit_orders(nbits):
    if nbits == 4:
        return [(3, 2, 1, 0), (2, 3, 0, 1), (1, 3, 2, 0), (0, 2, 3, 1)]
    return [tuple((nbits - 1 - p - t) % nbits for t in range(nbits)) for p in range(PARTS)]


def exchange_kernel(axis, nbits, reduce, gather, x_ref, out_ref, send_sem, recv_sem, *scratch):
    me = lax.axis_index(axis)
    bits = [lax.rem(lax.div(me, 2**b), 2) for b in range(nbits)]
    partner = [me + (1 - 2 * bits[b]) * 2**b for b in range(nbits)]
    orders = bit_orders(nbits)
    rows = (x_ref if not reduce else out_ref if not gather else x_ref).shape[-2] // PARTS
    span = [pl.ds(p * rows, rows) for p in range(PARTS)]

    def index(p, free, flip=None):
        lead = []
        for b in reversed(range(nbits)):
            if b in free:
                lead.append(slice(None))
            else:
                lead.append(1 - bits[b] if b == flip else bits[b])
        return tuple(lead) + (span[p], slice(None))

    def own(p):
        return index(p, ()) if gather else (span[p], slice(None))

    barrier = pltpu.get_barrier_semaphore()
    for b in range(nbits):
        pl.semaphore_signal(
            barrier, inc=1, device_id={axis: partner[b]}, device_id_type=pl.DeviceIdType.MESH
        )
    pl.semaphore_wait(barrier, nbits)

    def start(p, step, source, target, b):
        copy = pltpu.make_async_remote_copy(
            src_ref=source,
            dst_ref=target,
            send_sem=send_sem.at[p, step],
            recv_sem=recv_sem.at[p, step],
            device_id={axis: partner[b]},
            device_id_type=pl.DeviceIdType.MESH,
        )
        copy.start()
        return copy

    live = [None] * PARTS
    step = 0
    if reduce:
        acc, arrived = scratch[0], scratch[1:]

        def landing(p, t):
            return (slice(None),) * (nbits - 1 - t) + (span[p], slice(None))

        def add(p, t):
            live[p].wait()
            keep = index(p, orders[p][: nbits - 1 - t])
            source = x_ref if t == 0 else acc
            value = source[keep] + arrived[t][landing(p, t)]
            if t == nbits - 1:
                out_ref[own(p)] = value
            else:
                acc[keep] = value

        for t in range(nbits):
            for p in range(PARTS):
                if t > 0:
                    add(p, t - 1)
                b = orders[p][nbits - 1 - t]
                source = x_ref if t == 0 else acc
                live[p] = start(
                    p,
                    step,
                    source.at[index(p, orders[p][: nbits - 1 - t], b)],
                    arrived[t].at[landing(p, t)],
                    b,
                )
            step += 1
    for t in range(nbits if gather else 0):
        for p in range(PARTS):
            if t > 0:
                live[p].wait()
            elif reduce:
                add(p, nbits - 1)
            else:
                out_ref[own(p)] = x_ref[span[p], :]
            piece = out_ref.at[index(p, orders[p][:t])]
            live[p] = start(p, step, piece, piece, orders[p][t])
        step += 1
    for p in range(PARTS):
        if gather:
            live[p].wait()
        else:
            add(p, nbits - 1)


def exchange(x, axis, collective_id, reduce, gather):
    n = lax.axis_size(axis)
    nbits = n.bit_length() - 1
    width = x.shape[1]
    block = x.shape[0] // n if reduce else x.shape[0]
    whole = (2,) * nbits + (block, width)
    scratch = []
    if reduce:
        scratch.append(pltpu.VMEM(whole, jnp.float32))
        for t in range(nbits):
            scratch.append(pltpu.VMEM((2,) * (nbits - 1 - t) + (block, width), jnp.float32))
    steps = nbits * (int(reduce) + int(gather))
    out = pl.pallas_call(
        functools.partial(exchange_kernel, axis, nbits, reduce, gather),
        out_shape=jax.ShapeDtypeStruct(whole if gather else (block, width), jnp.float32),
        in_specs=[pl.BlockSpec(memory_space=pltpu.VMEM)],
        out_specs=pl.BlockSpec(memory_space=pltpu.VMEM),
        scratch_shapes=[
            pltpu.SemaphoreType.DMA((PARTS, steps)),
            pltpu.SemaphoreType.DMA((PARTS, steps)),
        ]
        + scratch,
        compiler_params=pltpu.CompilerParams(
            collective_id=collective_id, has_side_effects=True, vmem_limit_bytes=24 << 20
        ),
    )(x.reshape(whole) if reduce else x)
    return out.reshape(-1, width)


F32, BF16 = jnp.float32, jnp.bfloat16
MESH = pl.DeviceIdType.MESH
FEAT_TILE = 256
NBITS = 4
STREAMS = ((0, 64), (64, 64))
STRANDS = (
    (
        (((0, 1, 2, 3), 8), ((1, 0, 2, 3), 8), ((0, 2, 3, 1), 8), ((2, 1, 0, 3), 8)),
        (((0, 1, 2, 3), (2, 1, 0), 8), ((1, 0, 2, 3), (2, 0, 1), 8), ((0, 2, 3, 1), (3, 2, 0), 8), ((2, 1, 0, 3), (0, 1, 2), 8)),
        (((3, 2, 1, 0), 8), ((3, 2, 0, 1), 8), ((1, 3, 2, 0), 8), ((3, 0, 1, 2), 8)),
    ),
    (
        (((0, 1, 2, 3), 8), ((1, 0, 2, 3), 8), ((1, 2, 3, 0), 8), ((2, 0, 1, 3), 8)),
        (((0, 1, 2, 3), (2, 1, 0), 8), ((1, 0, 2, 3), (2, 0, 1), 8), ((1, 2, 3, 0), (3, 2, 1), 8), ((2, 0, 1, 3), (1, 0, 2), 8)),
        (((3, 2, 1, 0), 8), ((3, 2, 0, 1), 8), ((0, 3, 2, 1), 8), ((3, 1, 0, 2), 8)),
    ),
)
MOST = max(len(parts) for strand in STRANDS for parts in strand)
SCHEDULE = (
    0, 0, 0, 0, 0, 100, 100, 11, 100, 12, 13, 14, 100, 22, 21, 24, 23, 111, 11, 100, 13, 113, 112,
    114, 121, 122, 12, 13, 22, 124, 123, 24, 23, 14, 11, 112, 21, 113, 122, 12, 111, 22, 114, 124,
    14, 123, 121, 13, 23, 24, 112, 11, 10, 21, 113, 12, 10, 10, 122, 114, 22, 124, 111, 14, 10, 23,
    121, 123, 24, 113, 112, 21, 122, 114, 124, 111, 10, 20, 20, 20, 20, 20, 110, 110, 110, 110, 121,
    110, 11, 120, 120, 12, 13, 14, 123, 120, 120, 120, 22, 24, 21, 23, 114, 111, 13, 112, 113, 11,
    12, 124, 14, 23, 121, 122, 13, 22, 113, 11, 24, 12, 123, 112, 21, 124, 23, 114, 14, 22, 111,
    122, 113, 121, 13, 11, 24, 123, 23, 124, 12, 114, 112, 14, 21, 113, 111, 22, 122, 13, 121, 24,
    14, 11, 123, 12, 23, 22, 124, 24, 114, 14, 123, 13, 112, 11, 10, 12, 21, 10, 10, 124, 22, 113,
    23, 24, 111, 114, 122, 121, 13, 123, 12, 14, 10, 10, 112, 21, 11, 10, 10, 22, 113, 124, 23, 24,
    111, 112, 114, 122, 21, 121, 11, 13, 20, 20, 20, 20, 12, 20, 20, 14, 123, 113, 111, 110, 110,
    110, 122, 124, 112, 13, 21, 20, 121, 14, 114, 11, 120, 120, 120, 12, 120, 110, 110, 123, 111,
    110, 110, 13, 23, 122, 120, 120, 21, 22, 14, 24, 121, 120, 11, 113, 12, 111, 112, 0, 0, 0, 13,
    114, 21, 13, 24, 23, 22, 123, 14, 121, 0, 11, 122, 12, 124, 11, 14, 12, 114, 113, 111, 21, 112,
    24, 0, 22, 123, 23, 0, 0, 124, 121, 122, 114, 113, 21, 111, 24, 100, 0, 21, 22, 24, 112, 22,
    123, 0, 0, 0, 100, 100, 124, 23, 0, 114, 122, 23, 114, 113, 121, 0, 0, 0, 0, 0, 0, 113, 112,
    111, 124, 112, 0, 0, 0, 0, 0, 0, 100, 0, 111, 124, 123, 123, 121, 100, 100, 100, 100, 122, 121,
    122, 100, 100, 100, 100, 100, 100, 100, 100, 100, 100, 100, 100, 100, 100, 100, 100, 100, 0,
    0, 0, 0, 0, 100, 100, 11, 12, 13, 100, 14, 22, 21, 100, 24, 23, 111, 13, 11, 100, 113, 112, 121,
    122, 12, 114, 13, 22, 123, 24, 124, 14, 112, 23, 21, 11, 122, 111, 113, 12, 121, 22, 114, 13,
    124, 123, 24, 14, 23, 112, 11, 10, 21, 113, 12, 122, 114, 124, 22, 10, 111, 10, 23, 123, 121,
    24, 14, 10, 113, 112, 21, 10, 122, 114, 20, 20, 20, 20, 123, 124, 111, 20, 121, 110, 110, 110,
    110, 110, 11, 120, 120, 120, 120, 12, 14, 13, 120, 22, 24, 21, 23, 114, 111, 13, 112, 11, 113,
    124, 14, 23, 121, 122, 12, 13, 11, 22, 113, 123, 24, 21, 112, 23, 114, 124, 12, 14, 111, 22,
    11, 122, 121, 113, 13, 123, 24, 21, 23, 112, 114, 124, 12, 111, 14, 113, 11, 22, 122, 13, 121,
    123, 12, 14, 24, 11, 10, 21, 22, 23, 123, 112, 13, 12, 14, 10, 114, 10, 24, 124, 21, 11, 111,
    22, 113, 23, 122, 112, 13, 12, 121, 114, 124, 123, 24, 21, 20, 20, 20, 14, 10, 10, 111, 10, 10,
    112, 22, 113, 122, 121, 124, 23, 123, 114, 21, 111, 11, 13, 110, 110, 110, 12, 24, 20, 14, 20,
    20, 20, 113, 112, 122, 124, 121, 120, 120, 120, 120, 13, 111, 123, 114, 110, 110, 14, 23, 110,
    11, 21, 110, 22, 12, 24, 122, 120, 120, 121, 120, 13, 14, 21, 23, 11, 111, 113, 0, 22, 112, 12,
    24, 114, 0, 0, 123, 121, 13, 122, 124, 14, 0, 21, 13, 0, 11, 113, 12, 14, 11, 12, 123, 23, 22,
    124, 111, 0, 0, 112, 24, 121, 114, 122, 21, 113, 21, 123, 23, 124, 23, 24, 0, 112, 22, 24, 122,
    22, 0, 0, 0, 0, 113, 111, 113, 124, 121, 124, 0, 0, 0, 0, 0, 0, 114, 123, 0, 0, 0, 0, 0, 123,
    0, 0, 112, 111, 100, 100, 100, 112, 111, 122, 121, 114, 100, 100, 100, 100, 100, 122, 121, 114,
    100, 100, 100, 100, 100, 100, 100, 100, 100, 100, 100, 100, 100, 100, 100, 100, 100, 0, 0, 0,
    0, 0, 100, 100, 11, 12, 13, 100, 14, 22, 21, 100, 24, 23, 111, 13, 11, 100, 113, 112, 121, 122,
    12, 114, 13, 22, 123, 24, 124, 14, 112, 23, 21, 11, 122, 111, 113, 12, 121, 22, 114, 13, 124,
    123, 24, 14, 23, 112, 11, 10, 21, 113, 12, 122, 114, 124, 22, 10, 111, 10, 23, 123, 121, 24,
    14, 10, 113, 112, 21, 10, 122, 114, 20, 20, 20, 20, 123, 124, 111, 20, 121, 110, 110, 110, 110,
    110, 11, 120, 120, 120, 120, 12, 14, 13, 120, 22, 24, 21, 23, 114, 111, 13, 112, 11, 113, 124,
    14, 23, 121, 122, 12, 13, 11, 22, 113, 123, 24, 21, 112, 23, 114, 124, 12, 14, 111, 22, 11, 122,
    121, 113, 13, 123, 24, 21, 23, 112, 114, 124, 12, 111, 14, 113, 11, 22, 122, 13, 121, 123, 12,
    14, 24, 11, 10, 21, 22, 23, 123, 112, 13, 12, 14, 10, 114, 10, 24, 124, 21, 11, 111, 22, 113,
    23, 122, 112, 13, 12, 121, 114, 124, 123, 24, 21, 20, 20, 20, 14, 10, 10, 111, 10, 10, 112, 22,
    113, 122, 121, 124, 23, 123, 114, 21, 111, 11, 13, 110, 110, 110, 12, 24, 20, 14, 20, 20, 20,
    113, 112, 122, 124, 121, 120, 120, 120, 120, 13, 111, 123, 114, 110, 110, 14, 23, 110, 11, 21,
    110, 22, 12, 24, 122, 120, 120, 121, 120, 13, 14, 21, 23, 11, 111, 113, 0, 22, 112, 12, 24, 114,
    0, 0, 123, 121, 13, 122, 124, 14, 0, 21, 13, 0, 11, 113, 12, 14, 11, 12, 123, 23, 22, 124, 111,
    0, 0, 112, 24, 121, 114, 122, 21, 113, 21, 123, 23, 124, 23, 24, 0, 112, 22, 24, 122, 22, 0,
    0, 0, 0, 113, 111, 113, 124, 121, 124, 0, 0, 0, 0, 0, 0, 114, 123, 0, 0, 0, 0, 0, 123, 0, 0,
    112, 111, 100, 100, 100, 112, 111, 122, 121, 114, 100, 100, 100, 100, 100, 122, 121, 114, 100,
    100, 100, 100, 100, 100, 100, 100, 100, 100, 100, 100, 100, 100, 100, 100, 100, 0, 100,
)
MADE = ((1, 1), (1, 0), (0, 1), (0, 0))
READY = (1, 2, 3, 3)
USED = ((0, 0), (0, 1), (1, 0), (1, 1))


def dot(a, b, b_dim):
    return lax.dot_general(a, b, (((1,), (b_dim,)), ((), ())), preferred_element_type=F32)


def split(x):
    high = x.astype(BF16)
    return high, (x - high.astype(F32)).astype(BF16)


def needed(last_bit, dx, dy, halves):
    if last_bit == 0:
        return 1 if not dx else 2 if halves and not dy else 3
    if last_bit == 1:
        return 1 if not dy else 2 if halves and not dx else 3
    return 2 if halves and not dx else 3


def fused_kernel(
    samples_hbm, factor_hbm, targets_ref, sol_ref, res_ref,
    rows_vmem, factor_f32, factor_hi, factor_lo, res16, grad, grad_in, term, term_in, image, update,
    change, change_in, load_sem, factor_sem, send_sem, recv_sem, core_send, core_recv,
):
    me = lax.axis_index("row")
    col = lax.axis_index("col")
    bits = [lax.rem(lax.div(me, 2**b), 2) for b in range(NBITS)]
    partner = [me + (1 - 2 * bits[b]) * 2**b for b in range(NBITS)]
    relaxation = 1.0 / lax.axis_size("col")

    def block(z, dx, dy):
        lead = (z // 2, z % 2, 1 - bits[1] if dy else bits[1], 1 - bits[0] if dx else bits[0])
        return lead, ((lead[0] * 2 + lead[1]) * 2 + lead[2]) * 2 + lead[3]

    def load(flat):
        start = pl.multiple_of(flat * FEAT_TILE, FEAT_TILE)
        return pltpu.make_async_copy(
            samples_hbm.at[:, pl.ds(start, FEAT_TILE)], rows_vmem.at[flat], load_sem.at[flat]
        )

    for dx, dy in MADE:
        for z in range(4):
            load(block(z, dx, dy)[1]).start()
    factor_load = pltpu.make_async_copy(factor_hbm, factor_f32, factor_sem)
    factor_load.start()

    barrier = pltpu.get_barrier_semaphore()
    for b in range(NBITS):
        pl.semaphore_signal(barrier, inc=1, device_id={"row": partner[b]}, device_id_type=MESH)
    pl.semaphore_signal(barrier, inc=1, device_id={"col": 1 - col}, device_id_type=MESH)

    for i in range(0, targets_ref.shape[0], FEAT_TILE):
        tile = targets_ref[i : i + FEAT_TILE, :].T
        res_ref[:, i : i + FEAT_TILE] = tile
        res16[:, i : i + FEAT_TILE] = tile.astype(BF16)
    sol_ref[...] = jnp.zeros_like(sol_ref)
    pl.semaphore_wait(barrier, NBITS + 1)

    def index(rows, free, flip=None, halves=None):
        lead = []
        for b in reversed(range(NBITS)):
            if halves is not None and b == halves[0]:
                lead.append(1 - bits[b] if halves[1] else bits[b])
            elif b in free:
                lead.append(slice(None))
            else:
                lead.append(1 - bits[b] if b == flip else bits[b])
        return tuple(lead) + (rows, slice(None))

    own = tuple(bits[b] for b in reversed(range(NBITS)))

    def remote(source, target, b, s, phase, p, t):
        copy = pltpu.make_async_remote_copy(
            src_ref=source, dst_ref=target,
            send_sem=send_sem.at[s, phase, p, t], recv_sem=recv_sem.at[s, phase, p, t],
            device_id={"row": partner[b]}, device_id_type=MESH,
        )
        copy.start()
        return copy

    def landed(free, span):
        return (slice(None),) * len(free) + (span, slice(None))

    threads = {}
    done = set()
    ready = set()

    def spawn(name, thread):
        threads[name] = thread
        resume(name)

    def resume(name):
        try:
            next(threads[name])
        except StopIteration:
            del threads[name]

    def halve(buf, landing, order, span, s, phase, p, t):
        free = order[t + 1 :]
        return remote(
            buf.at[index(span, free, order[t])], landing[t].at[landed(free, span)], order[t], s, phase, p, t
        )

    def add(buf, landing, order, span, t):
        free = order[t + 1 :]
        keep = index(span, free)
        buf[keep] = buf[keep] + landing[t][landed(free, span)]

    def scatter_part(s, rnd, q, p, order, span, copy):
        for t in range(NBITS):
            yield
            copy.wait()
            add(grad, grad_in, order, span, t)
            if t < NBITS - 1:
                copy = halve(grad, grad_in, order, span, s, 0, slot_of(q, p), t + 1)
        done.add((s, rnd, 0, q, p))

    def reduce_part(s, rnd, q, p, order, rest, span, copy):
        at = slot_of(q, p)
        last = order[NBITS - 1 :]
        for t in range(NBITS - 1):
            yield
            copy.wait()
            add(term, term_in, order, span, t)
            if t < NBITS - 2:
                copy = halve(term, term_in, order, span, s, 1, at, t + 1)
        pair = index(span, last)
        copy = remote(term.at[pair], term_in[NBITS - 1].at[landed(last, span)], last[0], s, 1, at, NBITS - 1)
        yield
        copy.wait()
        image[pair] = term[pair] + term_in[NBITS - 1][landed(last, span)]
        for u, b in enumerate(rest):
            piece = image.at[index(span, last + rest[:u])]
            copy = remote(piece, piece, b, s, 2, at, u)
            if u == len(rest) - 1:
                done.add((s, rnd, 2, q, p, 1))
            yield
            copy.wait()
        done.add((s, rnd, 2, q, p, 3))

    def gather_part(s, rnd, q, p, order, span):
        at = slot_of(q, p)
        for t in range(NBITS - 1):
            piece = update.at[index(span, order[:t])]
            copy = remote(piece, piece, order[t], s, 3, at, t)
            yield
            copy.wait()
        last = order[NBITS - 1]
        across = 1 if last == 0 else 0
        copies = []
        for h in range(2):
            piece = update.at[index(span, order[: NBITS - 1], None, (across, h))]
            copies.append(remote(piece, piece, last, s, 3, at, NBITS - 1 + h))
        done.add((s, rnd, 3, q, p, 1))
        for h in range(2):
            yield
            copies[h].wait()
            done.add((s, rnd, 3, q, p, 2 + h))

    def need(flag):
        assert flag in done

    def slot_of(q, p):
        return q * MOST + p

    def placed(parts, lo):
        out = []
        for part in parts:
            out.append(part[:-1] + (pl.ds(lo, part[-1]),))
            lo += part[-1]
        return out

    def strand(s, rnd, q, lo):
        scatter, reduce, gather = STRANDS[q]
        width = sum(part[-1] for part in scatter)
        rows = slice(lo, lo + width)
        for p in range(len(scatter)):
            yield
            need((s, rnd, 0, q, p))
        own_grad = grad[own + (rows, slice(None))]
        if rnd > 0:
            own_grad = own_grad - ridge_weight * sol_ref[own + (rows, slice(None))]
        g_hi, g_lo = split(own_grad)
        g_both = jnp.concatenate([g_hi, g_lo], axis=0)
        if rnd == 0 and not ready:
            ready.add(0)
            factor_load.wait()
            for i in range(16):
                f_hi, f_lo = split(factor_f32[i * FEAT_TILE : (i + 1) * FEAT_TILE, :])
                factor_hi[i] = f_hi
                factor_lo[i] = f_lo

        for g, (dx, dy) in enumerate(MADE):
            for z in range(4):
                lead, flat = block(z, dx, dy)
                both = dot(g_both, factor_hi[flat], 1)
                term[lead + (rows, slice(None))] = (
                    both[:width] + both[width:] + dot(g_hi, factor_lo[flat], 1)
                )
            for p, (order, rest, span) in enumerate(placed(reduce, lo)):
                if READY[order[0]] == g:
                    copy = halve(term, term_in, order, span, s, 1, slot_of(q, p), 0)
                    spawn((s, q, p), reduce_part(s, rnd, q, p, order, rest, span, copy))
            if g == 1:
                yield

        seen = set()
        total = jnp.zeros((width, FEAT_TILE), F32)
        for dx, dy in USED:
            for p, part in enumerate(reduce):
                event = needed(part[1][-1], dx, dy, False)
                if (p, event) not in seen:
                    seen.add((p, event))
                    yield
                    need((s, rnd, 2, q, p, event))
            for z in range(4):
                lead, flat = block(z, dx, dy)
                i_hi, i_lo = split(image[lead + (rows, slice(None))])
                both = dot(jnp.concatenate([i_hi, i_lo], axis=0), factor_hi[flat], 0)
                total = total + both[:width] + both[width:] + dot(i_hi, factor_lo[flat], 0)
        update[own + (rows, slice(None))] = total
        for p, (order, span) in enumerate(placed(gather, lo)):
            spawn((s, q, p), gather_part(s, rnd, q, p, order, span))

    def stream(s, rnd):
        lo, width = STREAMS[s]
        rows = slice(lo, lo + width)
        starts = [lo]
        for scatter, _, _ in STRANDS:
            starts.append(starts[-1] + sum(part[-1] for part in scatter))

        for g, (dx, dy) in enumerate(MADE):
            for z in range(4):
                lead, flat = block(z, dx, dy)
                if rnd == 0 and s == 0:
                    load(flat).wait()
                grad[lead + (rows, slice(None))] = dot(res16[rows, :], rows_vmem[flat], 0)
            for q, (scatter, _, _) in enumerate(STRANDS):
                for p, (order, span) in enumerate(placed(scatter, starts[q])):
                    if READY[order[0]] == g:
                        copy = halve(grad, grad_in, order, span, s, 0, slot_of(q, p), 0)
                        spawn((s, q, p), scatter_part(s, rnd, q, p, order, span, copy))
            if g < 3:
                yield
        for q in range(len(STRANDS)):
            spawn((s, q), strand(s, rnd, q, starts[q]))

        seen = set()
        for dx, dy in USED:
            yield
            for q, (_, _, gather) in enumerate(STRANDS):
                for p, part in enumerate(gather):
                    event = needed(part[0][-1], dx, dy, True)
                    if (q, p, event) not in seen:
                        seen.add((q, p, event))
                        yield
                        need((s, rnd, 3, q, p, event))
            acc = None if (dx, dy) == USED[0] else change[rows, :]
            for z in range(4):
                lead, flat = block(z, dx, dy)
                at = lead + (rows, slice(None))
                value = update[at]
                sol_ref[at] = sol_ref[at] + relaxation * value
                product = dot(value.astype(BF16), rows_vmem[flat], 1)
                acc = product if acc is None else acc + product
            change[rows, :] = acc

        slot = rnd % 2
        copy = pltpu.make_async_remote_copy(
            src_ref=change.at[rows, :], dst_ref=change_in.at[slot, rows, :],
            send_sem=core_send.at[s, slot], recv_sem=core_recv.at[s, slot],
            device_id={"col": 1 - col}, device_id_type=MESH,
        )
        copy.start()
        yield
        copy.wait()
        residual = res_ref[rows, :] - relaxation * (change[rows, :] + change_in[slot, rows, :])
        res_ref[rows, :] = residual
        if rnd < ROUNDS - 1:
            res16[rows, :] = residual.astype(BF16)

    def whole(s):
        for rnd in range(ROUNDS):
            yield from stream(s, rnd)

    for s in range(len(STREAMS)):
        threads[(s,)] = whole(s)
    for number in SCHEDULE:
        s, q, p = number // 100, number // 10 % 10, number % 10
        resume((s, q - 1, p - 1) if p else (s, q - 1) if q else (s,))
    assert not threads


def fused(samples, targets, factor):
    count, width = samples.shape
    lanes = targets.shape[1]
    blocks = (2,) * NBITS + (lanes, FEAT_TILE)
    n_blocks = width // FEAT_TILE

    def landing(sizes):
        return [pltpu.VMEM((2,) * free + (lanes, FEAT_TILE), F32) for free in sizes]

    n_streams = len(STREAMS)
    n_parts = MOST * len(STRANDS)
    vmem = pl.BlockSpec(memory_space=pltpu.VMEM)
    anywhere = pl.BlockSpec(memory_space=pl.ANY)
    copies = pltpu.SemaphoreType.DMA((n_streams, 4, n_parts, NBITS + 1))
    sol, res = pl.pallas_call(
        fused_kernel,
        out_shape=(
            jax.ShapeDtypeStruct(blocks, F32),
            jax.ShapeDtypeStruct((lanes, count), F32),
        ),
        in_specs=[anywhere, anywhere, vmem],
        out_specs=(vmem, vmem),
        scratch_shapes=[
            pltpu.VMEM((n_blocks, count, FEAT_TILE), BF16),
            pltpu.VMEM(factor.shape, F32),
            pltpu.VMEM((n_blocks, FEAT_TILE, FEAT_TILE), BF16),
            pltpu.VMEM((n_blocks, FEAT_TILE, FEAT_TILE), BF16),
            pltpu.VMEM((lanes, count), BF16),
            pltpu.VMEM(blocks, F32),
            landing((3, 2, 1, 0)),
            pltpu.VMEM(blocks, F32),
            landing((3, 2, 1, 1)),
            pltpu.VMEM(blocks, F32),
            pltpu.VMEM(blocks, F32),
            pltpu.VMEM((lanes, count), F32),
            pltpu.VMEM((2, lanes, count), F32),
            pltpu.SemaphoreType.DMA((n_blocks,)),
            pltpu.SemaphoreType.DMA(()),
            copies,
            copies,
            pltpu.SemaphoreType.DMA((n_streams, 2)),
            pltpu.SemaphoreType.DMA((n_streams, 2)),
        ],
        compiler_params=pltpu.CompilerParams(
            collective_id=0, has_side_effects=True, vmem_limit_bytes=58 << 20
        ),
    )(samples, factor, targets)
    solution = jnp.swapaxes(sol.reshape(n_blocks, lanes, FEAT_TILE), 1, 2).reshape(width, lanes)
    return solution, res.T


def run_group(samples, residual, inverse, own_rows, offset, relaxation):
    solution = jnp.zeros((samples.shape[1], residual.shape[1]), jnp.float32)
    for sweep in range(ROUNDS):
        res16 = residual.astype(jnp.bfloat16)
        part_grad = jnp.einsum("rb,rk->bk", samples, res16, preferred_element_type=jnp.float32)
        own_solution = lax.dynamic_slice_in_dim(solution, offset, own_rows, 0)
        grad_own = exchange(part_grad, "row", 0, True, False) - ridge_weight * own_solution
        term = jnp.dot(inverse, grad_own, precision=lax.Precision.HIGH)
        image = exchange(term, "row", 1, True, True)
        update_own = jnp.einsum("bc,bk->ck", inverse, image, precision=lax.Precision.HIGH)
        update = exchange(update_own, "row", 2, False, True)
        solution = solution + relaxation * update
        change = jnp.dot(samples, update.astype(jnp.bfloat16), preferred_element_type=jnp.float32)
        residual = residual - relaxation * exchange(change, "col", 3, True, True)
    return (solution, residual)


def per_device(samples, targets, factor_inv):
    inverse = factor_inv[0]
    if lax.axis_size("row") == 2**NBITS and inverse.shape[1] == FEAT_TILE and lax.axis_size("col") == 2:
        return fused(samples, targets, inverse)
    own_rows = inverse.shape[1]
    offset = lax.axis_index("row") * own_rows
    relaxation = 1.0 / lax.axis_size("col")
    solution, residual = run_group(samples, targets, inverse, own_rows, offset, relaxation)
    return (solution, residual)


def solution(mesh):
    in_specs = (P("row", "col"), P("row", None), P("col", None, "row"))
    out_specs = (P("col", None), P("row", None))
    return jax.shard_map(
        per_device, mesh=mesh, in_specs=in_specs, out_specs=out_specs, check_vma=False
    )
```
